32 devices in a mesh: req: 2 (over y), ep: 16 (over z, x, core).
Axes of the slice: x: 2, y: 2, z: 4, core: 2. Of those that a mesh axis runs over, the one named last changes fastest.
Arguments:
- queries: bfloat16 [256, 64, 576], P(('req', 'ep')), may hold values from -7 to 7
- latent_cache: bfloat16 [32, 512, 576], P(('req', 'ep')), may hold values from -3 to 3
- new_latents: bfloat16 [256, 576], P(('req', 'ep')), may hold values from -4 to 4
- parents: int32 [16, 16], replicated, may hold values from 0 to 14, as said below
- cache_len: int32 [16], replicated, may hold values from 128 to 1024
- tokens: bfloat16 [256, 7168], P(('req', 'ep')), may hold values from -6 to 6
- route_ids: int32 [256, 8], P(('req', 'ep')), may hold values from 0 to 15, all different within a row; in each aligned block of 8 rows (0 to 7, 8 to 15, ...) at most 5 rows name the same one
- route_scores: float32 [256, 8], P(('req', 'ep')), may hold values from 0.05 to 1
- w_gate: bfloat16 [16, 7168, 2048], P('ep', None, 'req'), may hold values from -0.0625 to 0.0625
- w_up: bfloat16 [16, 7168, 2048], P('ep', None, 'req'), may hold values from -0.0625 to 0.0625
- w_down: bfloat16 [16, 2048, 7168], P('ep', 'req'), may hold values from -0.125 to 0.125
Outputs:
- attention_out: bfloat16 [256, 64, 512], P(('req', 'ep'))
- moe_out: bfloat16 [256, 7168], P(('req', 'ep'))
The draws below stay inside these ranges and needn't reach their ends.
Inputs may be any that keep to these rules, and one draw needn't show every extreme that they name: `route_ids`: each row names 8 different experts. Among the 8 tokens of one device (aligned blocks of 8 rows) no expert is named by more than 5 tokens, a bound that some block reaches. parents[q, 0] = 0 and parents[q, j] < j for j >= 1.
All inputs are finite; a program needn't handle non-finite values.
Results may differ from the reference program's by a relative error of at most 0.015.
Values may be sent and summed in bfloat16 or wider, within the bound.
No kernel may reach another device: no remote copies, remote signals or barrier semaphores. Data moves between devices by JAX's collectives and lax.ppermute only.
A program may use at most 128 MiB of HBM per device.

```python
import math
import jax
import jax.numpy as jnp
import numpy as np
from jax import lax

D = 7168
FF = 2048
VDIM = 512
TOP = 8
HEADS = 64
NODES = 16
CTX = 1024
LAT = 576
TOK_DEV = 8
REQUESTS = 16
TOKENS = 256
EXPERTS = 16
FF_DEV = 1024
MOST = 5
N_REQ = 2


def joint_cache(key):
    cache_key = jax.random.fold_in(jax.random.fold_in(key, 11), 0)
    cache_shape = (REQUESTS * 2, CTX // 2, LAT)
    cache_vals = jnp.clip(jax.random.normal(cache_key, cache_shape, jnp.float32), -3.0, 3.0)
    return cache_vals


def draw_latent_cache(key, part):
    return joint_cache(key).astype(jnp.bfloat16)


def draw_queries(key, part):
    query_key = jax.random.fold_in(key, 23)
    query_shape = (REQUESTS, NODES, HEADS, LAT)
    values = jnp.clip(jax.random.normal(query_key, query_shape, jnp.float32), -6.0, 6.0)
    return values.reshape(TOKENS, HEADS, LAT).astype(jnp.bfloat16)


def draw_parents(key, part):
    offsets = jax.random.randint(jax.random.fold_in(key, 31), (REQUESTS, NODES), 0, 4)
    node_ids = jnp.arange(NODES, dtype=jnp.int32)
    parent_ids = jnp.maximum(node_ids[None, :] - 1 - offsets, 0)
    return parent_ids.at[0, NODES - 1].set(NODES - 2).astype(jnp.int32)


def draw_cache_len(key, part):
    lengths = jax.random.randint(jax.random.fold_in(key, 37), (REQUESTS,), CTX // 8, CTX + 1)
    return lengths.at[0].set(CTX).at[1].set(CTX // 8).astype(jnp.int32)


def shard_levels(stream_key, dims, cuts, least, top_value):
    def one(dim, shards_of):
        draws = jax.random.uniform(jax.random.fold_in(jax.random.fold_in(stream_key, 6), dim), (shards_of,), jnp.float32, least / len(cuts), top_value / len(cuts))
        return jnp.repeat(jnp.exp(draws), dims[dim] // shards_of).reshape((-1,) + (1,) * (len(dims) - dim - 1))

    loudness = one(*cuts[0])
    for cut in cuts[1:]:
        loudness = loudness * one(*cut)
    return loudness


def routed_block(own_key, own, number, rows, amount, top, reach, skew):
    order = jax.random.permutation(own_key, amount)
    crowded, common = shares(amount, rows * top, reach, skew, True), shares(amount, rows * top, reach, skew, False)
    places = jnp.arange(amount)

    def named(sizes, rotation):
        used = int((sizes > 0).sum())
        fixed = max(1, used // 4)
        moved = fixed + (places - fixed + rotation * (used - fixed)) % max(1, amount - fixed)
        return jnp.zeros((amount,), jnp.int32).at[order[jnp.where(places < fixed, places, moved)]].set(jnp.asarray(sizes, jnp.int32))

    sizes = jnp.where(number % 4 == 0, named(crowded, number // 4), named(common, number - number // 4 - 1))
    mixed = jax.random.permutation(jax.random.fold_in(own, 3), amount)
    donor, taker = mixed[0:amount // 2 * 2:2], mixed[1:amount // 2 * 2:2]
    margin = jnp.minimum(sizes[donor] - 1, reach - sizes[taker]) // 2
    margin = jnp.where((donor == order[0]) | (taker == order[0]) | (sizes[taker] == 0), 0, jnp.maximum(margin, 0))
    moved = jax.random.randint(jax.random.fold_in(own, 4), (amount // 2,), 0, 1 << 20) % (margin + 1)
    sizes = sizes.at[donor].add(-moved).at[taker].add(moved)
    labels = jnp.searchsorted(jnp.cumsum(sizes), jnp.arange(rows * top), side="right").astype(jnp.int32)
    table = labels.reshape(top, rows).T
    table = table[jax.random.permutation(jax.random.fold_in(own, 1), rows)]
    rotation = jax.random.randint(jax.random.fold_in(own, 2), (rows, 1), 0, top)
    return jnp.take_along_axis(table, (jnp.arange(top)[None, :] + rotation) % top, axis=1)


def shares(amount, total, limit, lean, full):
    portions = [(1 << 20) // math.isqrt(standing ** lean) + 1 for standing in range(1, amount + 1)]
    largest = limit if full else min(limit, max(-(-total // amount), total * portions[0] // sum(portions)))
    least = 1 if total - largest >= amount - 1 else 0
    given, surplus = [largest] + [least] * (amount - 1), total - largest - least * (amount - 1)
    while surplus > 0:
        movable = [i for i in range(1, amount) if given[i] < largest] or [i for i in range(1, amount) if given[i] < limit]
        pool, remaining = sum([portions[i] for i in movable]), surplus
        for i in movable:
            more = min(limit - given[i], max(1, remaining * portions[i] // pool), surplus)
            given[i] = given[i] + more
            surplus = surplus - more
    return np.array(given)


def centred(rng, extent, width, most, cuts=(), held_as=jnp.bfloat16):
    result = width * jax.random.normal(rng, extent, jnp.float32)
    if cuts:
        result = result * shard_levels(rng, extent, cuts, -0.22, 0.18)
    return jnp.clip(result, -most, most).astype(held_as)


def setup_inputs(seed: int = 0) -> dict:
    splits = jax.random.split(jax.random.key(seed), 12)
    queries = draw_queries(jax.random.fold_in(splits[11], 71), 0)
    latent_cache = draw_latent_cache(jax.random.fold_in(splits[11], 71), 0)
    new_latents = centred(splits[2], (TOKENS, LAT), 1.0, 4.0, ((0, 32),))
    parents = draw_parents(jax.random.fold_in(splits[11], 71), 0)
    cache_len = draw_cache_len(jax.random.fold_in(splits[11], 71), 0)
    tokens = centred(splits[5], (TOKENS, D), 1.0, 6.0, ((0, 32),))
    route_ids_keys = jax.random.split(jax.random.fold_in(splits[6], 1), TOKENS // TOK_DEV)
    route_ids_turns = jax.random.permutation(jax.random.fold_in(splits[6], 3), TOKENS // TOK_DEV)
    route_ids = jax.vmap(lambda own, number: routed_block(jax.random.fold_in(splits[6], 2), own, number, TOK_DEV, EXPERTS, TOP, MOST, 2))(route_ids_keys, route_ids_turns).reshape((TOKENS, TOP))
    route_scores = jnp.clip(0.05 + 0.95 * jax.random.uniform(splits[7], (TOKENS, TOP), jnp.float32) ** shard_levels(splits[7], (TOKENS, TOP), ((0, 32),), -0.2, 0.2), 0.05, 1.0)
    w_gate = centred(splits[8], (EXPERTS, D, FF), D ** -0.5, 0.0625, ((0, 16), (2, 2)))
    w_up = centred(splits[9], (EXPERTS, D, FF), D ** -0.5, 0.0625, ((0, 16), (2, 2)))
    w_down = centred(splits[10], (EXPERTS, FF, D), FF ** -0.5, 0.125, ((0, 16), (1, 2)))
    return dict(queries=queries, latent_cache=latent_cache, new_latents=new_latents, parents=parents, cache_len=cache_len, tokens=tokens, route_ids=route_ids, route_scores=route_scores, w_gate=w_gate, w_up=w_up, w_down=w_down)


score_scale = 192.0 ** -0.5
route_scale = 2.5


def ancestor_table(parent_row):
    node_count = parent_row.shape[0]
    node_ids = jnp.arange(node_count, dtype=jnp.int32)
    current = node_ids
    visible = node_ids[:, None] == node_ids[None, :]
    for repeat in range(node_count):
        current = parent_row[current]
        visible = visible | (current[:, None] == node_ids[None, :])
    return visible


def attend_request(operands):
    query_rows, cache_rows, fresh_rows, parent_row, length = operands
    context = cache_rows.shape[0] * cache_rows.shape[1]
    key_rows = jnp.concatenate([cache_rows.reshape(context, cache_rows.shape[2]), fresh_rows], axis=0)
    scores = jnp.einsum("nhl,kl->nhk", query_rows.astype(jnp.float32), key_rows.astype(jnp.float32)) * score_scale
    cached = jnp.arange(context, dtype=jnp.int32) < length
    tree_vis = ancestor_table(parent_row)
    visible = jnp.concatenate([jnp.broadcast_to(cached[None, :], (tree_vis.shape[0], context)), tree_vis], axis=1)
    masked = jnp.where(visible[:, None, :], scores, -jnp.inf)
    row_max = jnp.max(masked, axis=-1, keepdims=True)
    shifted = jnp.exp(masked - row_max)
    attn_probs = (shifted / jnp.sum(shifted, axis=-1, keepdims=True)).astype(jnp.bfloat16)
    value_rows = key_rows[:, :VDIM]
    return jnp.einsum("nhk,kv->nhv", attn_probs.astype(jnp.float32), value_rows.astype(jnp.float32)).astype(jnp.bfloat16)


def reference(queries, latent_cache, new_latents, parents, cache_len, tokens, route_ids, route_scores, w_gate, w_up, w_down):
    query_group = queries.reshape(REQUESTS, NODES, HEADS, LAT)
    cache_group = latent_cache.reshape(REQUESTS, 2, CTX // 2, LAT)
    fresh_group = new_latents.reshape(REQUESTS, NODES, LAT)
    attended = lax.map(attend_request, (query_group, cache_group, fresh_group, parents, cache_len))
    attention_out = attended.reshape(TOKENS, HEADS, VDIM)

    route_weight = route_scale * route_scores / jnp.sum(route_scores, axis=1, keepdims=True)
    blocks = TOKENS // TOK_DEV
    block_ids = route_ids.reshape(blocks, TOK_DEV * TOP)
    onehot = (block_ids[:, :, None] == jnp.arange(EXPERTS, dtype=jnp.int32)[None, None, :]).astype(jnp.int32)
    slot_rank = jnp.sum(jnp.cumsum(onehot, axis=1) * onehot, axis=2) - 1
    slot_of = block_ids * (blocks * MOST) + jnp.arange(blocks, dtype=jnp.int32)[:, None] * MOST + slot_rank
    token_of_pair = jnp.arange(TOKENS * TOP, dtype=jnp.int32) // TOP
    table_size = EXPERTS * blocks * MOST
    token_table = jnp.zeros((table_size,), jnp.int32).at[slot_of.reshape(-1)].set(token_of_pair)
    weight_table = jnp.zeros((table_size,), jnp.float32).at[slot_of.reshape(-1)].set(route_weight.reshape(-1))
    token_table = token_table.reshape(EXPERTS, blocks * MOST)
    weight_table = weight_table.reshape(EXPERTS, blocks * MOST)

    def one_expert(running, operands):
        gate_mat, up_mat, down_mat, token_rows, row_weights = operands
        picked = tokens[token_rows]
        gate_val = jnp.dot(picked, gate_mat, preferred_element_type=jnp.float32)
        up_val = jnp.dot(picked, up_mat, preferred_element_type=jnp.float32)
        hidden = (jax.nn.silu(gate_val) * up_val).astype(jnp.bfloat16)
        pieces = hidden.reshape(hidden.shape[0], N_REQ, FF_DEV)
        partial_value = jnp.einsum("rnf,nfd->nrd", pieces.astype(jnp.float32), down_mat.reshape(N_REQ, FF_DEV, D).astype(jnp.float32)).astype(jnp.bfloat16)
        expert_out = jnp.sum(partial_value.astype(jnp.float32), axis=0)
        return running.at[token_rows].add(expert_out * row_weights[:, None]), None

    running, unused = lax.scan(one_expert, jnp.zeros((TOKENS, D), jnp.float32), (w_gate, w_up, w_down, token_table, weight_table))
    moe_out = running.astype(jnp.bfloat16)
    return attention_out, moe_out
```

```python
import functools

import jax
import jax.numpy as jnp
from jax import lax
from jax.experimental import pallas as pl
from jax.experimental.pallas import tpu as pltpu
from jax.sharding import PartitionSpec as P

VDIM = 512
AXES = ("req", "ep")
NEG = -1e30

score_scale = 192.0 ** (-0.5)
route_scale = 2.5


def swap(block, count, partner):
    return lax.ppermute(block, AXES, [(i, partner(i)) for i in range(count)])


def pack_kernel(ep_count, tokens_ref, ids_ref, scores_ref, mine_ref, theirs_ref):
    core = lax.axis_index("ep") % 2
    half = tokens_ref.shape[1] // 2
    extra = mine_ref.shape[1] - half
    scores = scores_ref[...]
    weight = route_scale * scores / jnp.sum(scores, axis=1, keepdims=True)
    ids = ids_ref[...]
    lane = lax.broadcasted_iota(jnp.int32, (ids.shape[0], extra), 1)
    expert = jnp.where(lane >= ep_count, lane - ep_count, lane)
    dense = jnp.zeros(lane.shape, jnp.float32)
    for k in range(ids.shape[1]):
        dense = dense + jnp.where(ids[:, k : k + 1] == expert, weight[:, k : k + 1], 0.0)
    high = dense.astype(jnp.bfloat16)
    low = (dense - high.astype(jnp.float32)).astype(jnp.bfloat16)
    packed = jnp.where(
        lane < ep_count, high.astype(jnp.float32), jnp.where(lane < 2 * ep_count, low.astype(jnp.float32), 0.0)
    ).astype(jnp.bfloat16)
    first = tokens_ref[:, :half]
    second = tokens_ref[:, half:]
    even = core == 0
    mine_ref[:, :half] = jnp.where(even, first, second)
    theirs_ref[:, :half] = jnp.where(even, second, first)
    mine_ref[:, half:] = packed
    theirs_ref[:, half:] = packed


def pack(tokens, route_ids, route_scores, ep_count, extra):
    rows, width = tokens.shape
    out = jax.ShapeDtypeStruct((rows, width // 2 + extra), jnp.bfloat16)
    return pl.pallas_call(
        functools.partial(pack_kernel, ep_count),
        out_shape=(out, out),
        name="pack",
    )(tokens, route_ids, route_scores)


def attention_kernel(
    where_ref, parents_ref, length_ref, q_ref, own_ref, other_ref, fresh_ref, other_fresh_ref, out_ref, line_ref
):
    half_index, request = where_ref[0], where_ref[1]
    nodes = line_ref.shape[0]
    tok_dev = nodes // 2
    rows = q_ref.shape[0]
    heads = rows // (tok_dev // pl.num_programs(0))
    length = length_ref[request]
    line_ref[0] = 1
    for node in range(1, nodes):
        line_ref[node] = (1 << node) | line_ref[parents_ref[request, node]]
    span = own_ref.shape[1]
    queries = q_ref[...]
    column = lax.broadcasted_iota(jnp.int32, (1, span), 1)
    dims = (((1,), (0,)), ((), ()))
    flipped = (((1,), (1,)), ((), ()))

    def masked(keys_ref, start):
        scores = lax.dot_general(queries, keys_ref[...], dims, preferred_element_type=jnp.float32) * score_scale
        return jnp.where(column + start < length, scores, NEG)

    scores_own = masked(own_ref, half_index * span)
    scores_other = masked(other_ref, (1 - half_index) * span)

    def tree(keys_ref, first_key):
        scores = lax.dot_general(queries, keys_ref[...], flipped, preferred_element_type=jnp.float32) * score_scale
        key = first_key + lax.broadcasted_iota(jnp.int32, (heads, tok_dev), 1)
        pieces = []
        for t in range(rows // heads):
            node = half_index * tok_dev + pl.program_id(0) * (rows // heads) + t
            ancestors = line_ref[node]
            pieces.append(
                jnp.where((jnp.full(key.shape, ancestors, jnp.int32) >> key) & 1 == 1, scores[t * heads : (t + 1) * heads], NEG)
            )
        return jnp.concatenate(pieces, axis=0)

    scores_fresh = tree(fresh_ref, half_index * tok_dev)
    scores_fresh_other = tree(other_fresh_ref, (1 - half_index) * tok_dev)
    parts = (scores_own, scores_other, scores_fresh, scores_fresh_other)
    top = functools.reduce(jnp.maximum, [jnp.max(part, axis=1, keepdims=True) for part in parts])
    weights = [jnp.exp(part - top) for part in parts]
    total = functools.reduce(jnp.add, [jnp.sum(part, axis=1, keepdims=True) for part in weights])
    vdim = out_ref.shape[1]
    out = lax.dot_general(
        weights[0].astype(jnp.bfloat16), own_ref[:vdim, :], flipped, preferred_element_type=jnp.float32
    )
    out += lax.dot_general(
        weights[1].astype(jnp.bfloat16), other_ref[:vdim, :], flipped, preferred_element_type=jnp.float32
    )
    out += lax.dot_general(
        weights[2].astype(jnp.bfloat16), fresh_ref[:, :vdim], dims, preferred_element_type=jnp.float32
    )
    out += lax.dot_general(
        weights[3].astype(jnp.bfloat16), other_fresh_ref[:, :vdim], dims, preferred_element_type=jnp.float32
    )
    out_ref[...] = (out / total).astype(out_ref.dtype)


def attention(queries, own, other, fresh, other_fresh, parents, cache_len, half_index, request):
    tok_dev, heads, width = queries.shape
    rows = tok_dev * heads
    steps = 2
    whole = lambda array: pl.BlockSpec(array.shape, lambda i, *_: (0,) * array.ndim)
    out = pl.pallas_call(
        attention_kernel,
        out_shape=jax.ShapeDtypeStruct((rows, VDIM), jnp.bfloat16),
        grid_spec=pltpu.PrefetchScalarGridSpec(
            num_scalar_prefetch=3,
            grid=(steps,),
            in_specs=[
                pl.BlockSpec((rows // steps, width), lambda i, *_: (i, 0)),
                whole(own),
                whole(other),
                whole(fresh),
                whole(other_fresh),
            ],
            out_specs=pl.BlockSpec((rows // steps, VDIM), lambda i, *_: (i, 0)),
            scratch_shapes=[pltpu.SMEM((parents.shape[1],), jnp.int32)],
        ),
        cost_estimate=pl.CostEstimate(
            flops=2 * rows * 1040 * (width + VDIM), bytes_accessed=3 * 1024 * 1024, transcendentals=rows * 1040
        ),
        name="attention",
    )(
        jnp.stack([half_index, request]).astype(jnp.int32),
        parents,
        cache_len,
        queries.reshape(rows, width),
        own,
        other,
        fresh,
        other_fresh,
    )
    return out.reshape(tok_dev, heads, VDIM)


def gate_up_kernel(
    steps, ep_count, core_ref, mine_lo, mine_hi, other_lo, other_hi, side_lo, side_hi, gate_ref, up_ref, out_ref, gate_acc, up_acc
):
    step = pl.program_id(0)
    quarter = mine_lo.shape[0] // 2
    rows = mine_lo.shape[0]

    @pl.when(step == 0)
    def _():
        gate_acc[...] = jnp.zeros_like(gate_acc)
        up_acc[...] = jnp.zeros_like(up_acc)

    def add(start, block):
        at = pl.ds(start, block.shape[0])
        gate_acc[at, :] += jnp.dot(block, gate_ref[...], preferred_element_type=jnp.float32)
        up_acc[at, :] += jnp.dot(block, up_ref[...], preferred_element_type=jnp.float32)

    @pl.when(step < steps)
    def _():
        add(0, jnp.concatenate([mine_lo[...], mine_hi[...]], axis=0))

    @pl.when(step >= steps)
    def _():
        add(
            0,
            jnp.concatenate(
                [other_lo[:quarter, :], other_hi[:quarter, :], other_lo[quarter:, :], other_hi[quarter:, :]], axis=0
            ),
        )

    @pl.when(step == 2 * steps - 1)
    def _():
        expert = core_ref[1]
        for start, side in ((0, side_lo), (rows, side_hi)):
            at = pl.ds(start, rows)
            values = side[...].astype(jnp.float32)
            lane = lax.broadcasted_iota(jnp.int32, values.shape, 1)
            hit = (lane == expert) | (lane == expert + ep_count)
            weight = jnp.sum(jnp.where(hit, values, 0.0), axis=1, keepdims=True)
            gate = gate_acc[at, :]
            out_ref[at, :] = (gate / (1.0 + jnp.exp(-gate)) * up_acc[at, :] * weight).astype(out_ref.dtype)


def gate_up(place, mine_lo, mine_hi, other_lo, other_hi, w_gate, w_up, ep_count, half):
    rows, width = mine_lo.shape
    hidden = w_gate.shape[1]
    tile = half // 2
    steps = half // tile
    extra = width - half
    own = pl.BlockSpec((rows, tile), lambda k, p: (0, jnp.minimum(k, steps - 1)))
    other = pl.BlockSpec((rows, tile), lambda k, p: (0, jnp.maximum(k - steps, 0)))
    side = pl.BlockSpec((rows, extra), lambda k, p: (0, half // extra))
    weight = pl.BlockSpec((tile, hidden), lambda k, p: (jnp.where(k < steps, p[0] * steps + k, (1 - p[0]) * steps + k - steps), 0))
    return pl.pallas_call(
        functools.partial(gate_up_kernel, steps, ep_count),
        out_shape=jax.ShapeDtypeStruct((2 * rows, hidden), jnp.bfloat16),
        grid_spec=pltpu.PrefetchScalarGridSpec(
            num_scalar_prefetch=1,
            grid=(2 * steps,),
            in_specs=[own, own, other, other, side, side, weight, weight],
            out_specs=pl.BlockSpec((2 * rows, hidden), lambda k, p: (0, 0)),
            scratch_shapes=[pltpu.VMEM((2 * rows, hidden), jnp.float32)] * 2,
        ),
        compiler_params=pltpu.CompilerParams(vmem_limit_bytes=48 * 1024 * 1024),
        cost_estimate=pl.CostEstimate(
            flops=8 * rows * half * 2 * hidden, bytes_accessed=8 * half * hidden, transcendentals=2 * rows * hidden
        ),
        name="gate_up",
    )(place, mine_lo, mine_hi, other_lo, other_hi, mine_lo, mine_hi, w_gate, w_up)


def down_kernel(theirs, place_ref, hidden_ref, weight_ref, low_ref, high_ref):
    out = jnp.dot(hidden_ref[...], weight_ref[...], preferred_element_type=jnp.float32).astype(low_ref.dtype)
    rows = low_ref.shape[0]
    quarter = rows // 2
    if theirs:
        low_ref[:quarter, :] = out[:quarter]
        low_ref[quarter:, :] = out[rows : rows + quarter]
        high_ref[:quarter, :] = out[quarter:rows]
        high_ref[quarter:, :] = out[rows + quarter :]
    else:
        low_ref[...] = out[:rows]
        high_ref[...] = out[rows:]


def down(place, hidden, w_down, half, theirs):
    rows, depth = hidden.shape
    tile = half // 2
    steps = half // tile
    side = (lambda p: 1 - p[0]) if theirs else (lambda p: p[0])
    out = jax.ShapeDtypeStruct((rows // 2, half), jnp.bfloat16)
    out_spec = pl.BlockSpec((rows // 2, tile), lambda n, p: (0, n))
    return pl.pallas_call(
        functools.partial(down_kernel, theirs),
        out_shape=(out, out),
        grid_spec=pltpu.PrefetchScalarGridSpec(
            num_scalar_prefetch=1,
            grid=(steps,),
            in_specs=[
                pl.BlockSpec((rows, depth), lambda n, p: (0, 0)),
                pl.BlockSpec((depth, tile), lambda n, p: (0, side(p) * steps + n)),
            ],
            out_specs=(out_spec, out_spec),
        ),
        compiler_params=pltpu.CompilerParams(vmem_limit_bytes=32 * 1024 * 1024),
        cost_estimate=pl.CostEstimate(
            flops=2 * rows * depth * half, bytes_accessed=2 * depth * half, transcendentals=0
        ),
        name="down_theirs" if theirs else "down_mine",
    )(place, hidden, w_down)


def body(
    queries,
    latent_cache,
    new_latents,
    parents,
    cache_len,
    tokens,
    route_ids,
    route_scores,
    w_gate,
    w_up,
    w_down,
):
    ep_count = lax.axis_size("ep")
    count = lax.axis_size("req") * ep_count
    bits = count.bit_length() - 1
    assert count == 1 << bits and bits >= 4
    expert = lax.axis_index("ep")
    position = lax.axis_index("req") * ep_count + expert
    core = position % 2
    even = core == 0
    first, last = 2, 1 << (bits - 1)
    group = 1 << (bits - 3)

    def trade_pair(block):
        return swap(block, count, lambda i: i ^ 1)

    def trade_near(block):
        return swap(block, count, lambda i: i ^ (first if i % 2 == 0 else last))

    def trade_far(block):
        return swap(block, count, lambda i: i ^ (last if i % 2 == 0 else first))

    def trade_group(block, offset):
        return swap(block, count, lambda i: i ^ (offset * 4))

    half = tokens.shape[1] // 2
    extra = -(-2 * ep_count // 128) * 128
    place = jnp.stack([core, expert]).astype(jnp.int32)

    mine, theirs = pack(tokens, route_ids, route_scores, ep_count, extra)
    got = trade_pair(theirs)
    pair = jnp.concatenate([jnp.where(even, mine, got), jnp.where(even, got, mine)], axis=0)
    line = jnp.concatenate([pair] + [trade_group(pair, j) for j in range(1, group)], axis=0)
    low = jnp.concatenate([line, trade_near(line)], axis=0)
    high = trade_far(low)
    other_low = trade_pair(low)
    other_high = trade_pair(high)

    cache = jnp.swapaxes(latent_cache[0], 0, 1)
    other_cache, other_fresh = trade_pair(cache), trade_pair(new_latents)
    attention_out = attention(
        queries, cache, other_cache, new_latents, other_fresh, parents, cache_len, core, position // 2
    )

    hidden = gate_up(place, low, high, other_low, other_high, w_gate[0], w_up[0], ep_count, half)
    send_low, send_high = down(place, hidden, w_down[0], half, True)
    keep_low, keep_high = down(place, hidden, w_down[0], half, False)

    def add(*blocks):
        return functools.reduce(jnp.add, [block.astype(jnp.float32) for block in blocks])

    def rounded(*blocks):
        return add(*blocks).astype(jnp.bfloat16)

    back_high = trade_pair(send_high)
    back_low = trade_pair(send_low)
    far = trade_far(rounded(keep_high, back_high))
    quarter = keep_low.shape[0] // 2
    near = trade_near(rounded(keep_low[quarter:], back_low[quarter:], far[quarter:]))
    rows = quarter // group
    sums = rounded(keep_low[:quarter], back_low[:quarter], far[:quarter], near)
    parts = [sums[:rows]] + [trade_group(sums[j * rows : (j + 1) * rows], j) for j in range(1, group)]
    total = rounded(*parts)
    tok_dev = tokens.shape[0]
    keep = jnp.where(even, total[:tok_dev], total[tok_dev:])
    give = jnp.where(even, total[tok_dev:], total[:tok_dev])
    given = trade_pair(give)
    moe_out = jnp.concatenate([jnp.where(even, keep, given), jnp.where(even, given, keep)], axis=1)
    return (attention_out, moe_out)


def solution(mesh):
    placed = (
        P(("req", "ep"), None, None),
        P(("req", "ep"), None, None),
        P(("req", "ep"), None),
        P(),
        P(),
        P(("req", "ep"), None),
        P(("req", "ep"), None),
        P(("req", "ep"), None),
        P("ep", None, "req"),
        P("ep", None, "req"),
        P("ep", "req", None),
    )
    return jax.shard_map(
        body,
        mesh=mesh,
        in_specs=placed,
        out_specs=(P(("req", "ep"), None, None), P(("req", "ep"), None)),
        check_vma=False,
    )
```

```python
import functools

import jax
import jax.numpy as jnp
from jax import lax
from jax.experimental import pallas as pl
from jax.experimental.pallas import tpu as pltpu
from jax.sharding import PartitionSpec as P


VDIM = 512
AXES = ("req", "ep")
NEG = -1e30
OUT_CHUNKS = 2
BACK_CHUNKS = 2
AHEAD = 3
KERNEL_VMEM = 42 * 1024 * 1024
DOWN_VMEM = 16 * 1024 * 1024

score_scale = 192.0 ** (-0.5)
route_scale = 2.5


def swap(block, count, partner):
    return lax.ppermute(block, AXES, [(i, partner(i)) for i in range(count)])


VMEM = pl.BlockSpec(memory_space=pltpu.VMEM)
SMEM = pl.BlockSpec(memory_space=pltpu.SMEM)
HBM = pl.BlockSpec(memory_space=pltpu.HBM)


def pack_kernel(ep_count, tokens_ref, ids_ref, scores_ref, out_ref):
    width = tokens_ref.shape[1]
    extra = out_ref.shape[1] - width
    scores = scores_ref[...]
    weight = route_scale * scores / jnp.sum(scores, axis=1, keepdims=True)
    ids = ids_ref[...]
    lane = lax.broadcasted_iota(jnp.int32, (ids.shape[0], extra), 1)
    expert = jnp.where(lane >= ep_count, lane - ep_count, lane)
    dense = jnp.zeros(lane.shape, jnp.float32)
    for k in range(ids.shape[1]):
        dense = dense + jnp.where(ids[:, k : k + 1] == expert, weight[:, k : k + 1], 0.0)
    high = dense.astype(jnp.bfloat16).astype(jnp.float32)
    packed = jnp.where(lane < ep_count, high, jnp.where(lane < 2 * ep_count, dense - high, 0.0))
    out_ref[:, :width] = tokens_ref[...]
    out_ref[:, width:] = packed.astype(jnp.bfloat16)


def pack(tokens, route_ids, route_scores, ep_count, extra, chunk, width):
    rows = tokens.shape[0]
    return pl.pallas_call(
        functools.partial(pack_kernel, ep_count),
        grid=(1,),
        in_specs=[
            pl.BlockSpec((rows, width), lambda i: (0, chunk)),
            pl.BlockSpec(route_ids.shape, lambda i: (0, 0)),
            pl.BlockSpec(route_scores.shape, lambda i: (0, 0)),
        ],
        out_specs=pl.BlockSpec((rows, width + extra), lambda i: (0, 0)),
        out_shape=jax.ShapeDtypeStruct((rows, width + extra), jnp.bfloat16),
        name="pack",
    )(tokens, route_ids, route_scores)


def attention_kernel(
    where_ref, parents_ref, length_ref, q_ref, own_ref, other_ref, fresh_ref, other_fresh_ref, out_ref, line_ref
):
    half_index, request = where_ref[0], where_ref[1]
    nodes = line_ref.shape[0]
    tok_dev = nodes // 2
    rows = q_ref.shape[0]
    heads = rows // (tok_dev // pl.num_programs(0))
    length = length_ref[request]
    line_ref[0] = 1
    for node in range(1, nodes):
        line_ref[node] = (1 << node) | line_ref[parents_ref[request, node]]
    span = own_ref.shape[1]
    queries = q_ref[...]
    column = lax.broadcasted_iota(jnp.int32, (1, span), 1)
    dims = (((1,), (0,)), ((), ()))
    flipped = (((1,), (1,)), ((), ()))

    def masked(keys_ref, start):
        scores = lax.dot_general(queries, keys_ref[...], dims, preferred_element_type=jnp.float32) * score_scale
        return jnp.where(column + start < length, scores, NEG)

    scores_own = masked(own_ref, half_index * span)
    scores_other = masked(other_ref, (1 - half_index) * span)

    def tree(keys_ref, first_key):
        scores = lax.dot_general(queries, keys_ref[...], flipped, preferred_element_type=jnp.float32) * score_scale
        key = first_key + lax.broadcasted_iota(jnp.int32, (heads, tok_dev), 1)
        pieces = []
        for t in range(rows // heads):
            node = half_index * tok_dev + pl.program_id(0) * (rows // heads) + t
            ancestors = line_ref[node]
            pieces.append(
                jnp.where((jnp.full(key.shape, ancestors, jnp.int32) >> key) & 1 == 1, scores[t * heads : (t + 1) * heads], NEG)
            )
        return jnp.concatenate(pieces, axis=0)

    scores_fresh = tree(fresh_ref, half_index * tok_dev)
    scores_fresh_other = tree(other_fresh_ref, (1 - half_index) * tok_dev)
    parts = (scores_own, scores_other, scores_fresh, scores_fresh_other)
    top = functools.reduce(jnp.maximum, [jnp.max(part, axis=1, keepdims=True) for part in parts])
    weights = [jnp.exp(part - top) for part in parts]
    total = functools.reduce(jnp.add, [jnp.sum(part, axis=1, keepdims=True) for part in weights])
    vdim = out_ref.shape[1]
    out = lax.dot_general(
        weights[0].astype(jnp.bfloat16), own_ref[:vdim, :], flipped, preferred_element_type=jnp.float32
    )
    out += lax.dot_general(
        weights[1].astype(jnp.bfloat16), other_ref[:vdim, :], flipped, preferred_element_type=jnp.float32
    )
    out += lax.dot_general(
        weights[2].astype(jnp.bfloat16), fresh_ref[:, :vdim], dims, preferred_element_type=jnp.float32
    )
    out += lax.dot_general(
        weights[3].astype(jnp.bfloat16), other_fresh_ref[:, :vdim], dims, preferred_element_type=jnp.float32
    )
    out_ref[...] = (out / total).astype(out_ref.dtype)


def attention(queries, own, other, fresh, other_fresh, parents, cache_len, half_index, request):
    tok_dev, heads, width = queries.shape
    rows = tok_dev * heads
    steps = 2
    whole = lambda array: pl.BlockSpec(array.shape, lambda i, *_: (0,) * array.ndim)
    out = pl.pallas_call(
        attention_kernel,
        out_shape=jax.ShapeDtypeStruct((rows, VDIM), jnp.bfloat16),
        grid_spec=pltpu.PrefetchScalarGridSpec(
            num_scalar_prefetch=3,
            grid=(steps,),
            in_specs=[
                pl.BlockSpec((rows // steps, width), lambda i, *_: (i, 0)),
                whole(own),
                whole(other),
                whole(fresh),
                whole(other_fresh),
            ],
            out_specs=pl.BlockSpec((rows // steps, VDIM), lambda i, *_: (i, 0)),
            scratch_shapes=[pltpu.SMEM((parents.shape[1],), jnp.int32)],
        ),
        cost_estimate=pl.CostEstimate(
            flops=2 * rows * 1040 * (width + VDIM), bytes_accessed=3 * 1024 * 1024, transcendentals=rows * 1040
        ),
        name="attention",
    )(
        jnp.stack([half_index, request]).astype(jnp.int32),
        parents,
        cache_len,
        queries.reshape(rows, width),
        own,
        other,
        fresh,
        other_fresh,
    )
    return out.reshape(tok_dev, heads, VDIM)


def gate_up_kernel(chunk, width, ep_count, tile, *refs):
    place_ref, low_ref, high_ref, other_low_ref, other_high_ref, gate_hbm, up_hbm = refs[:7]
    slots, sems = refs[-2:]
    sums, outs = refs[7:-3] if ep_count else refs[7:-4], refs[-3:-2] if ep_count else refs[-4:-2]
    core = place_ref[0]
    rows = low_ref.shape[0]
    quarter = rows // 2
    starts = ((2 * chunk + core) * width, (2 * chunk + 1 - core) * width)
    order = [(side, i, k) for side in range(2) for i in range(2) for k in range(0, width, tile)]

    def fetch(n):
        side, i, k = order[n]
        source = (gate_hbm, up_hbm)[i]
        at = pl.ds(pl.multiple_of(starts[side] + k, 128), tile)
        return pltpu.make_async_copy(source.at[at, :], slots.at[n], sems.at[n])

    for n in range(min(AHEAD, len(order))):
        fetch(n).start()
    values = [None, None]
    for n, (side, i, k) in enumerate(order):
        if n + AHEAD < len(order):
            fetch(n + AHEAD).start()
        if side == 0:
            pieces = [low_ref[:, k : k + tile], high_ref[:, k : k + tile]]
        else:
            pieces = [
                other_low_ref[:quarter, k : k + tile],
                other_high_ref[:quarter, k : k + tile],
                other_low_ref[quarter:, k : k + tile],
                other_high_ref[quarter:, k : k + tile],
            ]
        fetch(n).wait()
        if quarter < 256:
            pieces = [jnp.concatenate(pieces, axis=0)]
        value = jnp.concatenate(
            [jnp.dot(piece, slots[n], preferred_element_type=jnp.float32) for piece in pieces], axis=0
        )
        if values[i] is None:
            values[i] = value + sums[i][...] if sums else value
        else:
            values[i] += value
    if not ep_count:
        outs[0][...], outs[1][...] = values
        return
    expert = place_ref[1]
    out_ref = outs[0]
    for start, side in ((0, low_ref), (rows, high_ref)):
        beside = side[:, width:].astype(jnp.float32)
        lane = lax.broadcasted_iota(jnp.int32, beside.shape, 1)
        hit = (lane == expert) | (lane == expert + ep_count)
        weight = jnp.sum(jnp.where(hit, beside, 0.0), axis=1, keepdims=True)
        gate = values[0][start : start + rows]
        up = values[1][start : start + rows]
        out_ref[start : start + rows, :] = (gate / (1.0 + jnp.exp(-gate)) * up * weight).astype(out_ref.dtype)


def gate_up(place, chunk, width, low, high, other_low, other_high, w_gate, w_up, sums, ep_count):
    rows, hidden = 2 * low.shape[0], w_gate.shape[1]
    total = jax.ShapeDtypeStruct((rows, hidden), jnp.float32)
    out_shape = jax.ShapeDtypeStruct((rows, hidden), jnp.bfloat16) if ep_count else (total, total)
    tile = width // 2 if width % 256 == 0 else width
    tiles = 4 * width // tile
    return pl.pallas_call(
        functools.partial(gate_up_kernel, chunk, width, ep_count, tile),
        out_shape=out_shape,
        in_specs=[SMEM] + [VMEM] * 4 + [HBM] * 2 + [VMEM] * len(sums),
        out_specs=VMEM if ep_count else (VMEM, VMEM),
        scratch_shapes=[pltpu.VMEM((tiles, tile, hidden), w_gate.dtype), pltpu.SemaphoreType.DMA((tiles,))],
        compiler_params=pltpu.CompilerParams(vmem_limit_bytes=KERNEL_VMEM),
        cost_estimate=pl.CostEstimate(
            flops=8 * rows * width * hidden, bytes_accessed=8 * width * hidden, transcendentals=0
        ),
    )(place, low, high, other_low, other_high, w_gate, w_up, *sums)


def down_kernel(chunk, theirs, place_ref, hidden_ref, weight_ref, low_ref, high_ref):
    core = place_ref[0]
    rows, width = low_ref.shape
    quarter = rows // 2
    side = 1 - core if theirs else core
    at = pl.ds(pl.multiple_of(side * (weight_ref.shape[1] // 2) + chunk * width, 128), width)
    out = jnp.dot(hidden_ref[...], weight_ref[:, at], preferred_element_type=jnp.float32).astype(low_ref.dtype)
    if theirs:
        low_ref[:quarter, :] = out[:quarter]
        low_ref[quarter:, :] = out[rows : rows + quarter]
        high_ref[:quarter, :] = out[quarter:rows]
        high_ref[quarter:, :] = out[rows + quarter :]
    else:
        low_ref[...] = out[:rows]
        high_ref[...] = out[rows:]


def down(place, chunk, width, hidden, w_down, theirs):
    rows, depth = hidden.shape
    out = jax.ShapeDtypeStruct((rows // 2, width), jnp.bfloat16)
    return pl.pallas_call(
        functools.partial(down_kernel, chunk, theirs),
        out_shape=(out, out),
        in_specs=[SMEM, VMEM, VMEM],
        out_specs=(VMEM, VMEM),
        compiler_params=pltpu.CompilerParams(vmem_limit_bytes=DOWN_VMEM),
        cost_estimate=pl.CostEstimate(
            flops=2 * rows * depth * width, bytes_accessed=2 * depth * width, transcendentals=0
        ),
    )(place, hidden, w_down)


def body(
    queries,
    latent_cache,
    new_latents,
    parents,
    cache_len,
    tokens,
    route_ids,
    route_scores,
    w_gate,
    w_up,
    w_down,
):
    ep_count = lax.axis_size("ep")
    count = lax.axis_size("req") * ep_count
    bits = count.bit_length() - 1
    assert count == 1 << bits and bits >= 4
    expert = lax.axis_index("ep")
    position = lax.axis_index("req") * ep_count + expert
    core = position % 2
    even = core == 0
    first, last = 2, 1 << (bits - 1)
    group = 1 << (bits - 3)

    def trade_pair(block):
        return swap(block, count, lambda i: i ^ 1)

    def trade_near(block):
        return swap(block, count, lambda i: i ^ (first if i % 2 == 0 else last))

    def trade_far(block):
        return swap(block, count, lambda i: i ^ (last if i % 2 == 0 else first))

    def trade_group(block, offset):
        return swap(block, count, lambda i: i ^ (offset * 4))

    full = tokens.shape[1]
    half = full // 2
    extra = -(-2 * ep_count // 128) * 128
    place = jnp.stack([core, expert]).astype(jnp.int32)
    tok_dev = tokens.shape[0]

    chunks = OUT_CHUNKS
    width = half // chunks

    def pick(block, own, span):
        part = jnp.where(even == own, block[:, :span], block[:, span : 2 * span])
        return part if block.shape[1] == 2 * span else jnp.concatenate([part, block[:, 2 * span :]], axis=1)

    lows, highs, other_lows, other_highs = [], [], [], []
    line = None

    def finish_near(line):
        low = jnp.concatenate([line, trade_near(line)], axis=0)
        high = trade_far(low)
        lows.append(low)
        highs.append(high)
        other_lows.append(trade_pair(low[:, :width]))
        other_highs.append(trade_pair(high[:, :width]))

    for j in range(chunks):
        if j == chunks - 1:
            block = pack(tokens, route_ids, route_scores, ep_count, extra, j, 2 * width)
        else:
            block = tokens[:, 2 * width * j : 2 * width * (j + 1)]
        rows_of = {k: trade_group(block, k) for k in order_of(group)}
        rows_of[0] = block
        if line is not None:
            rows_of, line = lax.optimization_barrier((rows_of, line))
            finish_near(line)
        stack = jnp.concatenate([rows_of[k] for k in range(group)], axis=0)
        mine, got = pick(stack, True, width), trade_pair(pick(stack, False, width))
        line = jnp.concatenate([jnp.where(even, mine, got), jnp.where(even, got, mine)], axis=0)
    finish_near(line)

    cache = jnp.swapaxes(latent_cache[0], 0, 1)
    other_cache, other_fresh = trade_pair(cache), trade_pair(new_latents)
    attention_out = attention(
        queries, cache, other_cache, new_latents, other_fresh, parents, cache_len, core, position // 2
    )

    sums = ()
    for j in range(chunks):
        sums = gate_up(
            place, j, width, lows[j], highs[j], other_lows[j], other_highs[j], w_gate[0], w_up[0], sums,
            ep_count if j == chunks - 1 else 0,
        )
    hidden = sums

    def rounded(*blocks):
        return functools.reduce(jnp.add, [block.astype(jnp.float32) for block in blocks]).astype(jnp.bfloat16)

    chunks = BACK_CHUNKS
    width = half // chunks
    outs = []
    for j in range(chunks):
        send_low, send_high = down(place, j, width, hidden, w_down[0], True)
        back_high, back_low = trade_pair(send_high), trade_pair(send_low)
        keep_low, keep_high = down(place, j, width, hidden, w_down[0], False)
        far = trade_far(rounded(keep_high, back_high))
        quarter = keep_low.shape[0] // 2
        near = trade_near(rounded(keep_low[quarter:], back_low[quarter:], far[quarter:]))
        line = rounded(keep_low[:quarter], back_low[:quarter], far[:quarter], near)
        first_rows, second_rows = line[: quarter // 2], line[quarter // 2 :]
        keep = jnp.where(even, first_rows, second_rows)
        given = trade_pair(jnp.where(even, second_rows, first_rows))
        whole = jnp.concatenate([jnp.where(even, keep, given), jnp.where(even, given, keep)], axis=1)
        parts = [whole[k * tok_dev : (k + 1) * tok_dev] for k in range(group)]
        moved = {k: trade_group(parts[k], k) for k in order_of(group)}
        outs.append(rounded(parts[0], *[moved[k] for k in range(1, group)]))
    moe_out = jnp.concatenate([out[:, :width] for out in outs] + [out[:, width:] for out in outs], axis=1)
    return (attention_out, moe_out)


def order_of(group):
    return [k for k in range(2, group)] + [1]


def solution(mesh):
    placed = (
        P(("req", "ep"), None, None),
        P(("req", "ep"), None, None),
        P(("req", "ep"), None),
        P(),
        P(),
        P(("req", "ep"), None),
        P(("req", "ep"), None),
        P(("req", "ep"), None),
        P("ep", None, "req"),
        P("ep", None, "req"),
        P("ep", "req", None),
    )
    return jax.shard_map(
        body,
        mesh=mesh,
        in_specs=placed,
        out_specs=(P(("req", "ep"), None, None), P(("req", "ep"), None)),
        check_vma=False,
    )
```
